256 devices in a mesh: gx: 16 (over y_lo, x, core), gy: 16 (over y_hi, z).
Axes of the slice: x: 4, y: 4 (y_hi: 2, y_lo: 2; y = y_hi * 2 + y_lo), z: 8, core: 2. Of those that a mesh axis runs over, the one named last changes fastest.
Arguments:
- operator: bfloat16 [16, 16, 2, 1536, 1536], P('gx', 'gy'), may hold values from -0.0390625 to 0.0390625
- incident: bfloat16 [16, 16, 2, 1536, 128], P('gx', 'gy'), may hold values from -6 to 6
- feed: bfloat16 [16, 16, 2, 1536], P('gx', 'gy'), may hold values from -24 to 24
- port_element: int32 [128], replicated, may hold values from 0 to 255
- positions: int32 [16, 16, 2], P('gx', 'gy'), may hold values from 0 to 122, as said below
Outputs:
- currents: bfloat16 [16, 16, 2, 1536, 128], P('gx', 'gy')
- fields: float32 [2048, 2, 128], P(('gx', 'gy'))
The draws below stay inside these ranges and needn't reach their ends.
Inputs may be any that keep to these rules, and one draw needn't show every extreme that they name: `positions`: element (c, r) lies at (c * 8 + j0, r * 8 + j1) with 0 <= j0, j1 < 3.
All inputs are finite; a program needn't handle non-finite values.
Results may differ from the reference program's by a relative error of at most 0.008.
Values may be sent and summed in bfloat16 or wider, within the bound.
No kernel may reach another device: no remote copies, remote signals or barrier semaphores. Data moves between devices by JAX's collectives and lax.ppermute only.
A program may use at most 64 MiB of HBM per device.

```python
import math
import jax
import jax.numpy as jnp
from jax import lax

FACE = 384
PORTS = 128
THETAS = 32
PHIS = 64
ITERS = 3
SPACING = 8
WAVE = 2
JITTER = 3
ORDER = 1536
COLS = 16
ROWS = 16
ELEMENTS = 256
ANGLES = 2048


def draw_positions(key, part):
    offsets = jax.random.randint(key, (COLS, ROWS, 2), 0, JITTER)
    column_base = jnp.broadcast_to((jnp.arange(COLS, dtype=jnp.int32) * SPACING)[:, None], (COLS, ROWS))
    row_base = jnp.broadcast_to((jnp.arange(ROWS, dtype=jnp.int32) * SPACING)[None, :], (COLS, ROWS))
    lattice = jnp.stack([column_base, row_base], axis=-1)
    return (lattice + offsets).astype(jnp.int32)


def plant(result, rng, low, top_value):
    longest = result.shape.index(max(result.shape))
    spots = []
    for shift in (0, 1):
        where = [jax.random.randint(jax.random.fold_in(rng, axis), (), 0, length) for axis, length in enumerate(result.shape)]
        where[longest] = (where[longest] + shift) % result.shape[longest]
        spots.append(tuple(where))
    return result.at[spots[0]].set(low).at[spots[1]].set(top_value)


def level_of(key, dims, shards, least, top_value):
    loudness = 1.0
    for position, shards_of in shards:
        heights = jax.random.uniform(jax.random.fold_in(jax.random.fold_in(key, 6), position), (shards_of,), jnp.float32, least / len(shards), top_value / len(shards))
        loudness = loudness * jnp.repeat(jnp.exp(heights), dims[position] // shards_of).reshape((-1,) + (1,) * (len(dims) - 1 - position))
    return loudness


def scatter_about(own_key, shape, scale, limit, cuts=(), kind=jnp.bfloat16):
    level = level_of(own_key, shape, cuts, -0.22, 0.18) if cuts else 1.0
    result = jax.random.normal(own_key, shape, jnp.float32) * scale * level
    return jnp.minimum(jnp.maximum(result, -limit), limit).astype(kind)


def setup_inputs(seed: int = 0) -> dict:
    splits = jax.random.split(jax.random.key(seed), 6)
    operator = scatter_about(splits[0], (COLS, ROWS, 2, ORDER, ORDER), (16 * ORDER) ** -0.5, 0.0390625, ((0, 16), (1, 16)))
    incident = scatter_about(splits[1], (COLS, ROWS, 2, ORDER, PORTS), 1.0, 6.0, ((0, 16), (1, 16)))
    feed = scatter_about(splits[2], (COLS, ROWS, 2, ORDER), 4.0, 24.0, ((0, 16), (1, 16)))
    port_element = plant(jax.random.randint(splits[3], (PORTS,), 0, ELEMENTS), jax.random.fold_in(splits[3], 1), 0, ELEMENTS - 1).astype(jnp.int32)
    positions = draw_positions(jax.random.fold_in(splits[5], 71), 0)
    return {"operator": operator, "incident": incident, "feed": feed, "port_element": port_element, "positions": positions}


TWO_PI = 2.0 * math.pi

def complex_product(mat_real, mat_imag, vec_real, vec_imag):
    width = vec_real.shape[1]
    stacked = jnp.concatenate([vec_real, vec_imag], axis=1)
    first = jnp.dot(mat_real, stacked, preferred_element_type=jnp.float32)
    second = jnp.dot(mat_imag, stacked, preferred_element_type=jnp.float32)
    return (first[:, :width] - second[:, width:], first[:, width:] + second[:, :width])

def directions(start, count):
    index = start + jnp.arange(count, dtype=jnp.int32)
    theta = ((index // PHIS).astype(jnp.float32) + 0.5) * (math.pi / (2.0 * THETAS))
    azimuth = (index % PHIS).astype(jnp.float32) * (TWO_PI / PHIS)
    return (jnp.sin(theta) * jnp.cos(azimuth), jnp.sin(theta) * jnp.sin(azimuth))

def basis_points(order):
    face_len = order // 4
    along = (jnp.arange(face_len, dtype=jnp.float32) + 0.5) * (SPACING / face_len)
    zeros = jnp.zeros((face_len,), jnp.float32)
    full = jnp.full((face_len,), float(SPACING), jnp.float32)
    return (jnp.concatenate([zeros, full, along, along]), jnp.concatenate([along, along, zeros, full]))

def field_rows(start, count, place_x, place_y, cur_real, cur_imag):
    order = cur_real.shape[0]
    width = cur_real.shape[1]
    points_x, points_y = basis_points(order)
    dir_x, dir_y = directions(start, count)
    psi = TWO_PI / WAVE * ((place_x + points_x)[None, :] * dir_x[:, None] + (place_y + points_y)[None, :] * dir_y[:, None])
    cosine = jnp.cos(psi).astype(jnp.bfloat16)
    sine = jnp.sin(psi).astype(jnp.bfloat16)
    stacked = jnp.concatenate([cur_real, cur_imag], axis=1)
    first = jnp.dot(cosine, stacked, preferred_element_type=jnp.float32)
    second = jnp.dot(sine, stacked, preferred_element_type=jnp.float32)
    real_part = first[:, :width] + second[:, width:]
    imag_part = first[:, width:] - second[:, :width]
    return jnp.stack([real_part, imag_part], axis=1)

def element_field(place_x, place_y, cur_real, cur_imag):
    block = 512 if ANGLES % 512 == 0 else ANGLES
    starts = jnp.arange(ANGLES // block, dtype=jnp.int32) * block
    pieces = lax.map(lambda begin: field_rows(begin, block, place_x, place_y, cur_real, cur_imag), starts)
    return pieces.reshape(ANGLES, 2, cur_real.shape[1])

def apply_element(pair):
    matrix, vector = pair
    real_part, imag_part = complex_product(matrix[0], matrix[1], vector[0], vector[1])
    return jnp.stack([real_part, imag_part])

def reference(operator, incident, feed, port_element, positions):
    elements = COLS * ROWS
    order = ORDER
    width = PORTS
    oper = operator.reshape(elements, 2, order, order)
    numbers = jnp.arange(elements, dtype=jnp.int32)
    selected = (port_element[None, :] == numbers[:, None]).astype(jnp.float32)
    rhs = (incident.reshape(elements, 2, order, width).astype(jnp.float32) + feed.reshape(elements, 2, order)[..., None].astype(jnp.float32) * selected[:, None, None, :]).astype(jnp.bfloat16)
    base = 0.5 * rhs.astype(jnp.float32) + lax.map(apply_element, (oper, rhs))
    current = base
    incoming = jnp.zeros((elements, 2, order, width), jnp.float32)
    for iteration in range(ITERS):
        outgoing = (2.0 * current - incoming).astype(jnp.bfloat16).reshape(COLS, ROWS, 2, 4, FACE, width)
        west = jnp.roll(outgoing[:, :, :, 1], 1, axis=0)
        east = jnp.roll(outgoing[:, :, :, 0], -1, axis=0)
        south = jnp.roll(outgoing[:, :, :, 3], 1, axis=1)
        north = jnp.roll(outgoing[:, :, :, 2], -1, axis=1)
        trace = jnp.stack([west, east, south, north], axis=3).reshape(elements, 2, order, width)
        incoming = trace.astype(jnp.float32)
        current = base + 0.5 * incoming + lax.map(apply_element, (oper, trace))
    currents = current.astype(jnp.bfloat16)
    places = positions.reshape(elements, 2).astype(jnp.float32)

    def accumulate(total, pair):
        place, cur = pair
        return (total + element_field(place[0], place[1], cur[0], cur[1]), None)
    total, _ = lax.scan(accumulate, jnp.zeros((ANGLES, 2, width), jnp.float32), (places, currents))
    fields = total * (1.0 / math.sqrt(order * elements))
    return (currents.reshape(COLS, ROWS, 2, order, width), fields)
```

```python
import math

import jax
import jax.numpy as jnp
import ml_dtypes
import numpy as np
from jax import lax
from jax.experimental import pallas as pl
from jax.experimental.pallas import tpu as pltpu
from jax.sharding import PartitionSpec as P

THETAS = 32
PHIS = 64
ITERS = 3
SPACING = 8
WAVE = 2
FACE = 384
PORTS = 128
ORDER = 4 * FACE
WIDE = 2 * PORTS
ANGLES = THETAS * PHIS
HALF_PHIS = PHIS // 2
STEP_THETAS = 4
STEPS = THETAS // 2 // STEP_THETAS
STEP_ROWS = STEP_THETAS * HALF_PHIS
STEP_DIRS = STEP_THETAS * PHIS


VMEM = pltpu.VMEM
HBM = pltpu.HBM
VMEM_LIMIT = 16 << 20
F32 = jnp.float32
BF16 = jnp.bfloat16


def theta_order():
    owner = np.arange(THETAS) // 2
    return [np.nonzero(owner % 2 == parity)[0] for parity in (0, 1)]


def face_tables():
    along = (np.arange(FACE) + 0.5) * (SPACING / FACE)
    sin_theta = np.sin((np.arange(THETAS) + 0.5) * (math.pi / (2.0 * THETAS)))
    sin_phi = np.sin(np.arange(HALF_PHIS) * (2.0 * math.pi / PHIS))
    angle = (2.0 * math.pi / WAVE) * (sin_theta[:, None] * sin_phi[None, :])[:, :, None] * along
    blocks = []
    for order in theta_order():
        for step in range(STEPS):
            part = angle[order[step * STEP_THETAS : (step + 1) * STEP_THETAS]]
            part = part.reshape(STEP_ROWS, FACE)
            blocks.append(np.concatenate([np.cos(part), np.sin(part)], axis=0))
    return np.stack(blocks).astype(ml_dtypes.bfloat16)


def direction_cosines():
    order = np.concatenate(theta_order())
    theta = (order + 0.5) * (math.pi / (2.0 * THETAS))
    azimuth = np.arange(PHIS) * (2.0 * math.pi / PHIS)
    dir_x = np.sin(theta)[:, None] * np.cos(azimuth)[None, :]
    dir_y = np.sin(theta)[:, None] * np.sin(azimuth)[None, :]
    whole = np.stack([dir_x.reshape(2 * STEPS, STEP_DIRS), dir_y.reshape(2 * STEPS, STEP_DIRS)], axis=1)
    return whole.astype(np.float32)


def swapped(vec):
    return jnp.concatenate([-vec[:, PORTS:], vec[:, :PORTS]], axis=1)


def faces_in_order():
    odd_x = lax.rem(lax.axis_index("gx"), 2)
    odd_y = lax.rem(lax.axis_index("gy"), 2)
    return (2 + odd_y, 3 - odd_y, odd_x, 1 - odd_x)


def face_rows(face):
    return pl.ds(pl.multiple_of(face * FACE, FACE), FACE)


def rows_product(oper_ref, rows, vec, vec_swapped):
    return jnp.dot(oper_ref[0, rows, :], vec, preferred_element_type=F32) + jnp.dot(
        oper_ref[1, rows, :], vec_swapped, preferred_element_type=F32
    )


def base_kernel(oper_hbm, incident_hbm, feed_hbm, ports_hbm, oper_ref, base_ref, *rest):
    outs, (incident, feed, ports, rhs_ref, sems, small_sems) = rest[:4], rest[4:]
    faces = faces_in_order()
    small = [
        pltpu.make_async_copy(source, target, small_sems.at[index])
        for index, (source, target) in enumerate(((incident_hbm, incident), (feed_hbm, feed), (ports_hbm, ports)))
    ]
    for copy in small:
        copy.start()
    large = []
    for index, face in enumerate(faces):
        rows = face_rows(face)
        large.append(
            pltpu.make_async_copy(oper_hbm.at[:, rows, :], oper_ref.at[:, rows, :], sems.at[index])
        )
        large[-1].start()
    for copy in small:
        copy.wait()
    myself = lax.axis_index("gx") * lax.axis_size("gy") + lax.axis_index("gy")
    selected = (ports[...] == myself).astype(F32).astype(BF16)
    blank = jnp.zeros_like(selected)
    select = jnp.concatenate(
        [jnp.concatenate([selected, blank], axis=1), jnp.concatenate([blank, selected], axis=1)], axis=0
    )
    fed = lax.dot_general(feed[...], select, (((0,), (0,)), ((), ())), preferred_element_type=F32)
    both = jnp.concatenate([incident[0], incident[1]], axis=1)
    rhs = (both.astype(F32) + fed).astype(BF16)
    rhs_ref[...] = rhs
    rhs_swapped = swapped(rhs)
    for index, face in enumerate(faces):
        rows = face_rows(face)
        large[index].wait()
        base = 0.5 * rhs_ref[rows, :].astype(F32) + rows_product(oper_ref, rows, rhs, rhs_swapped)
        base_ref[index] = base
        outs[index][...] = (2.0 * base).astype(BF16)


def gather_trace(faces, traces, trace_ref):
    for face, part in zip(faces, traces):
        trace_ref[face_rows(face), :] = part[...]
    trace = trace_ref[...]
    return trace, swapped(trace)


def step_kernel(oper_ref, base_ref, *rest):
    traces, outs, trace_ref = rest[:4], rest[4:8], rest[8]
    faces = faces_in_order()
    trace, trace_swapped = gather_trace(faces, traces, trace_ref)
    for index, face in enumerate(faces):
        coupled = rows_product(oper_ref, face_rows(face), trace, trace_swapped)
        outs[index][...] = (2.0 * (base_ref[index] + coupled)).astype(BF16)


def last_kernel(oper_ref, base_ref, *rest):
    traces, tables_ref, phases_ref = rest[:4], rest[4], rest[5]
    currents_hbm, vec_ref, out_ref, trace_ref, split_ref, sem = rest[6:]
    faces = faces_in_order()
    trace, trace_swapped = gather_trace(faces, traces, trace_ref)
    for index, face in enumerate(faces):
        rows = face_rows(face)
        coupled = rows_product(oper_ref, rows, trace, trace_swapped)
        currents = base_ref[index] + 0.5 * trace_ref[rows, :].astype(F32) + coupled
        currents = currents.astype(BF16)
        vec_ref[rows, :] = currents
        split_ref[0, rows, :] = currents[:, :PORTS]
        split_ref[1, rows, :] = currents[:, PORTS:]
    copy = pltpu.make_async_copy(split_ref, currents_hbm, sem)
    copy.start()
    field_steps(1 - lax.rem(lax.axis_index("gx"), 2), tables_ref, phases_ref, vec_ref, out_ref)
    copy.wait()


def own_field_kernel(tables_ref, phases_ref, vec_ref, out_ref):
    field_steps(lax.rem(lax.axis_index("gx"), 2), tables_ref, phases_ref, vec_ref, out_ref)


def field_steps(parity, tables_ref, phases_ref, vec_ref, out_ref):
    def body(step, carry):
        field_step(parity * STEPS + step, step, tables_ref, phases_ref, vec_ref, out_ref)
        return carry

    lax.fori_loop(0, STEPS, body, 0)


def field_step(block, step, tables_ref, phases_ref, vec_ref, out_ref):
    table = tables_ref[block]
    plus, minus = [], []
    for face in range(4):
        vec = vec_ref[pl.ds(face * FACE, FACE), :]
        both = jnp.dot(table, vec, preferred_element_type=F32)
        cos_real, cos_imag = both[:STEP_ROWS, :PORTS], both[:STEP_ROWS, PORTS:]
        sin_real, sin_imag = both[STEP_ROWS:, :PORTS], both[STEP_ROWS:, PORTS:]
        plus.append((cos_real + sin_imag, cos_imag - sin_real))
        minus.append((cos_real - sin_imag, cos_imag + sin_real))
    phases = phases_ref[block].T
    quarter = HALF_PHIS // 2
    for theta in range(STEP_THETAS):
        low = theta * HALF_PHIS
        high = low + HALF_PHIS

        def along_y(face, part):
            return (plus[face][part][low:high], minus[face][part][low:high])

        def along_x(face, part):
            first, second = plus[face][part][low:high], minus[face][part][low:high]
            return (
                jnp.concatenate([first[quarter:], second[:quarter]], axis=0),
                jnp.concatenate([second[quarter:], first[:quarter]], axis=0),
            )

        kinds = (along_y, along_y, along_x, along_x)
        terms = [[kind(face, part) for part in (0, 1)] for face, kind in enumerate(kinds)]
        for half in range(2):
            start = theta * PHIS + half * HALF_PHIS
            cols = phases[start : start + HALF_PHIS]
            shared = [terms[0][part][half] + terms[2][part][half] for part in (0, 1)]
            real, imag = 0.0, 0.0
            for column, (re, im) in (
                (0, shared),
                (2, (terms[1][0][half], terms[1][1][half])),
                (4, (terms[3][0][half], terms[3][1][half])),
            ):
                cos, sin = cols[:, column : column + 1], cols[:, column + 1 : column + 2]
                real = real + cos * re + sin * im
                imag = imag + cos * im - sin * re
            rows = pl.ds(pl.multiple_of(step * STEP_DIRS + start, HALF_PHIS), HALF_PHIS)
            out_ref[rows, :PORTS] = real.astype(BF16)
            out_ref[rows, PORTS:] = imag.astype(BF16)


def call(kernel, name, inputs, outputs, scratch, in_space, out_space, flops, moved):
    return pl.pallas_call(
        kernel,
        out_shape=outputs,
        in_specs=[pl.BlockSpec(memory_space=in_space.get(i, VMEM)) for i in range(len(inputs))],
        out_specs=[pl.BlockSpec(memory_space=out_space.get(i, VMEM)) for i in range(len(outputs))],
        scratch_shapes=scratch,
        compiler_params=pltpu.CompilerParams(vmem_limit_bytes=VMEM_LIMIT),
        cost_estimate=pl.CostEstimate(flops=flops, bytes_accessed=moved, transcendentals=0),
        name=name,
    )(*inputs)


def shape(dims, dtype):
    return jax.ShapeDtypeStruct(dims, dtype)


def pairings(count):
    near = [(i, i ^ 1) for i in range(count)]
    far = [(i, (i + 1) % count if i % 2 else (i - 1) % count) for i in range(count)]
    return far, near


def exchange(sends):
    received = []
    for axis, pair in (("gy", sends[:2]), ("gx", sends[2:])):
        for value, permutation in zip(pair, pairings(lax.axis_size(axis))):
            received.append(lax.ppermute(value, axis, permutation))
    return received


def phase_kernel(place_ref, cosines_ref, out_ref):
    factor = 1.0 / math.sqrt(ORDER * lax.axis_size("gx") * lax.axis_size("gy"))
    dir_x, dir_y = cosines_ref[:, 0], cosines_ref[:, 1]
    place_x, place_y = place_ref[0].astype(F32), place_ref[1].astype(F32)
    for index, (extra_x, extra_y) in enumerate(((0.0, 0.0), (SPACING, 0.0), (0.0, SPACING))):
        turns = ((place_x + extra_x) * dir_x + (place_y + extra_y) * dir_y) / WAVE
        angle = (turns - jnp.round(turns)) * (2.0 * math.pi)
        out_ref[:, 2 * index] = jnp.cos(angle) * factor
        out_ref[:, 2 * index + 1] = jnp.sin(angle) * factor
    for index in (6, 7):
        out_ref[:, index] = jnp.zeros((2 * STEPS, STEP_DIRS), F32)


def local(operator, incident, feed, port_element, positions):
    count_x, count_y = lax.axis_size("gx"), lax.axis_size("gy")
    product_flops = 4 * ORDER * ORDER * WIDE
    field_flops = 2 * ANGLES // 2 * FACE * WIDE * 4
    face_bf16 = shape((FACE, WIDE), BF16)
    wide_bf16 = shape((ORDER, WIDE), BF16)
    oper, base, *sends = call(
        base_kernel,
        "base",
        [
            pltpu.with_memory_space_constraint(value, HBM)
            for value in (operator[0, 0], incident[0, 0], feed[0, 0], port_element.reshape(1, PORTS))
        ],
        [shape((2, ORDER, ORDER), BF16), shape((4, FACE, WIDE), F32)] + [face_bf16] * 4,
        [
            VMEM((2, ORDER, PORTS), BF16),
            VMEM((2, ORDER), BF16),
            VMEM((1, PORTS), jnp.int32),
            VMEM((ORDER, WIDE), BF16),
            pltpu.SemaphoreType.DMA((4,)),
            pltpu.SemaphoreType.DMA((3,)),
        ],
        {0: HBM, 1: HBM, 2: HBM, 3: HBM},
        {},
        product_flops,
        10_000_000,
    )
    trace_scratch = VMEM((ORDER, WIDE), BF16)
    for _ in range(ITERS - 1):
        received = exchange(sends)
        sends = call(
            step_kernel,
            "step",
            (oper, base, *received),
            [face_bf16] * 4,
            [trace_scratch],
            {},
            {},
            product_flops,
            1_000_000,
        )
    received = exchange(sends)
    (phases,) = call(
        phase_kernel,
        "phases",
        (positions.reshape(2), jnp.asarray(direction_cosines())),
        [shape((2 * STEPS, 8, STEP_DIRS), F32)],
        [],
        {0: pltpu.SMEM},
        {},
        1_000_000,
        100_000,
    )
    tables = jnp.asarray(face_tables())
    half_field = shape((ANGLES // 2, WIDE), BF16)
    currents, vec, theirs = call(
        last_kernel,
        "last",
        (oper, base, *received, tables, phases),
        [shape((2, ORDER, PORTS), BF16), wide_bf16, half_field],
        [trace_scratch, VMEM((2, ORDER, PORTS), BF16), pltpu.SemaphoreType.DMA],
        {},
        {0: HBM},
        product_flops + field_flops,
        2_000_000,
    )
    theirs = lax.ppermute(theirs, "gx", [(i, i ^ 1) for i in range(count_x)])
    (mine,) = call(
        own_field_kernel, "own_field", (tables, phases, vec), [half_field], [], {}, {}, field_flops, 1_000_000
    )
    pair = (mine.astype(F32) + theirs.astype(F32)).astype(BF16)
    groups = [[i for i in range(count_x) if i % 2 == par] for par in (0, 1)]
    members = count_x // 2
    pieces = lax.all_to_all(pair, "gx", 0, 0, tiled=True, axis_index_groups=groups)
    column = jnp.sum(pieces.reshape(members, -1, WIDE).astype(F32), axis=0).astype(BF16)
    pieces = lax.all_to_all(column, "gy", 0, 0, tiled=True)
    pieces = pieces.reshape(count_y, -1, WIDE).astype(F32)
    fields = jnp.stack([jnp.sum(pieces[..., :PORTS], axis=0), jnp.sum(pieces[..., PORTS:], axis=0)], axis=1)
    return (currents[None, None], fields)


def solution(mesh):
    return jax.shard_map(
        local,
        mesh=mesh,
        in_specs=(
            P("gx", "gy", None, None, None),
            P("gx", "gy", None, None, None),
            P("gx", "gy", None, None),
            P(),
            P("gx", "gy", None),
        ),
        out_specs=(P("gx", "gy", None, None, None), P(("gx", "gy"), None, None)),
        check_vma=False,
    )
```

```python
import math

import jax
import jax.numpy as jnp
import ml_dtypes
import numpy as np
from jax import lax
from jax.experimental import pallas as pl
from jax.experimental.pallas import tpu as pltpu
from jax.sharding import PartitionSpec as P

THETAS = 32
PHIS = 64
ITERS = 3
SPACING = 8
WAVE = 2
FACE = 384
PORTS = 128
ORDER = 4 * FACE
WIDE = 2 * PORTS
ANGLES = THETAS * PHIS
HALF_PHIS = PHIS // 2
STEP_THETAS = 4
STEPS = THETAS // 2 // STEP_THETAS
STEP_ROWS = STEP_THETAS * HALF_PHIS
STEP_DIRS = STEP_THETAS * PHIS


VMEM = pltpu.VMEM
HBM = pltpu.HBM
VMEM_LIMIT = 16 << 20
UNROLL = 4
F32 = jnp.float32
BF16 = jnp.bfloat16


def theta_order():
    owner = np.arange(THETAS) // 2
    return [np.nonzero(owner % 2 == parity)[0] for parity in (0, 1)]


def face_tables():
    along = (np.arange(FACE) + 0.5) * (SPACING / FACE)
    sin_theta = np.sin((np.arange(THETAS) + 0.5) * (math.pi / (2.0 * THETAS)))
    sin_phi = np.sin(np.arange(HALF_PHIS) * (2.0 * math.pi / PHIS))
    angle = (2.0 * math.pi / WAVE) * (sin_theta[:, None] * sin_phi[None, :])[:, :, None] * along
    blocks = []
    for order in theta_order():
        for step in range(STEPS):
            part = angle[order[step * STEP_THETAS : (step + 1) * STEP_THETAS]]
            part = part.reshape(STEP_ROWS, FACE)
            blocks.append(np.concatenate([np.cos(part), np.sin(part)], axis=0))
    return np.stack(blocks).astype(ml_dtypes.bfloat16)


def direction_cosines():
    order = np.concatenate(theta_order())
    theta = (order + 0.5) * (math.pi / (2.0 * THETAS))
    azimuth = np.arange(PHIS) * (2.0 * math.pi / PHIS)
    dir_x = np.sin(theta)[:, None] * np.cos(azimuth)[None, :]
    dir_y = np.sin(theta)[:, None] * np.sin(azimuth)[None, :]
    whole = np.stack([dir_x.reshape(2 * STEPS, STEP_DIRS), dir_y.reshape(2 * STEPS, STEP_DIRS)], axis=1)
    return whole.astype(np.float32)


def swapped(vec):
    return jnp.concatenate([-vec[:, PORTS:], vec[:, :PORTS]], axis=1)


def faces_in_order():
    odd_x = lax.rem(lax.axis_index("gx"), 2)
    odd_y = lax.rem(lax.axis_index("gy"), 2)
    return (2 + odd_y, 3 - odd_y, odd_x, 1 - odd_x)


def face_rows(face):
    return pl.ds(pl.multiple_of(face * FACE, FACE), FACE)


def slot_product(oper_ref, slot, vec, vec_swapped):
    return jnp.dot(oper_ref[slot, 0], vec, preferred_element_type=F32) + jnp.dot(
        oper_ref[slot, 1], vec_swapped, preferred_element_type=F32
    )


def base_first_kernel(oper_hbm, incident_hbm, feed_hbm, ports_hbm, oper_ref, rhs_ref, base_ref, *rest):
    outs, (incident, feed, ports, sems, small_sems) = rest[:2], rest[2:]
    faces = faces_in_order()
    small = [
        pltpu.make_async_copy(source, target, small_sems.at[index])
        for index, (source, target) in enumerate(((incident_hbm, incident), (feed_hbm, feed), (ports_hbm, ports)))
    ]
    large = [
        pltpu.make_async_copy(oper_hbm.at[:, face_rows(face), :], oper_ref.at[slot], sems.at[slot])
        for slot, face in enumerate(faces)
    ]
    for copy in small + large[:2]:
        copy.start()
    for copy in small:
        copy.wait()
    myself = lax.axis_index("gx") * lax.axis_size("gy") + lax.axis_index("gy")
    selected = (ports[...] == myself).astype(F32).astype(BF16)
    blank = jnp.zeros_like(selected)
    select = jnp.concatenate(
        [jnp.concatenate([selected, blank], axis=1), jnp.concatenate([blank, selected], axis=1)], axis=0
    )
    fed = lax.dot_general(feed[...], select, (((0,), (0,)), ((), ())), preferred_element_type=F32)
    both = jnp.concatenate([incident[0], incident[1]], axis=1)
    rhs = (both.astype(F32) + fed).astype(BF16)
    rhs_ref[...] = rhs
    rhs_swapped = swapped(rhs)
    for index in range(2):
        large[index].wait()
        large[index + 2].start()
        base_slot(oper_ref, rhs_ref, rhs, rhs_swapped, faces, index, base_ref, outs, index)
    for copy in large[2:]:
        copy.wait()


def base_slot(oper_ref, rhs_ref, rhs, rhs_swapped, faces, slot, base_ref, outs, index):
    own = rhs_ref[face_rows(faces[slot]), :].astype(F32)
    base = 0.5 * own + slot_product(oper_ref, slot, rhs, rhs_swapped)
    base_ref[index] = base
    outs[index][...] = (2.0 * base).astype(BF16)


def base_second_kernel(oper_ref, rhs_ref, base_ref, *outs):
    faces = faces_in_order()
    rhs = rhs_ref[...]
    rhs_swapped = swapped(rhs)
    for index in range(2):
        base_slot(oper_ref, rhs_ref, rhs, rhs_swapped, faces, 2 + index, base_ref, outs, index)


def gather_trace(traces, trace_ref):
    for face, part in zip(faces_in_order(), traces):
        trace_ref[face_rows(face), :] = part[...]
    trace = trace_ref[...]
    return trace, swapped(trace)


def step_slots(oper_ref, base_ref, trace, trace_swapped, first, outs):
    for index in range(2):
        coupled = slot_product(oper_ref, first + index, trace, trace_swapped)
        outs[index][...] = (2.0 * (base_ref[index] + coupled)).astype(BF16)


def step_first_kernel(oper_ref, base_ref, *rest):
    traces, outs, trace_ref = rest[:4], rest[4:6], rest[6]
    trace, trace_swapped = gather_trace(traces, trace_ref)
    step_slots(oper_ref, base_ref, trace, trace_swapped, 0, outs)


def step_second_kernel(oper_ref, base_ref, trace_ref, *outs):
    trace = trace_ref[...]
    step_slots(oper_ref, base_ref, trace, swapped(trace), 2, outs)


def last_kernel(oper_ref, base_first_ref, base_second_ref, *rest):
    traces, tables_ref, phases_ref = rest[:4], rest[4], rest[5]
    currents_hbm, vec_ref, out_ref, trace_ref, split_ref, sem = rest[6:]
    trace, trace_swapped = gather_trace(traces, trace_ref)
    for slot, face in enumerate(faces_in_order()):
        rows = face_rows(face)
        base = (base_first_ref if slot < 2 else base_second_ref)[slot % 2]
        coupled = slot_product(oper_ref, slot, trace, trace_swapped)
        currents = (base + 0.5 * trace_ref[rows, :].astype(F32) + coupled).astype(BF16)
        vec_ref[rows, :] = currents
        split_ref[0, rows, :] = currents[:, :PORTS]
        split_ref[1, rows, :] = currents[:, PORTS:]
    copy = pltpu.make_async_copy(split_ref, currents_hbm, sem)
    copy.start()
    field_steps(1 - lax.rem(lax.axis_index("gx"), 2), tables_ref, phases_ref, vec_ref, out_ref)
    copy.wait()


def own_field_kernel(tables_ref, phases_ref, vec_ref, out_ref):
    field_steps(lax.rem(lax.axis_index("gx"), 2), tables_ref, phases_ref, vec_ref, out_ref)


def field_steps(parity, tables_ref, phases_ref, vec_ref, out_ref):
    def body(step, carry):
        field_step(parity * STEPS + step, step, tables_ref, phases_ref, vec_ref, out_ref)
        return carry

    lax.fori_loop(0, STEPS, body, 0, unroll=UNROLL)


def field_step(block, step, tables_ref, phases_ref, vec_ref, out_ref):
    table = tables_ref[block]
    plus, minus = [], []
    for face in range(4):
        vec = vec_ref[pl.ds(face * FACE, FACE), :]
        both = jnp.dot(table, vec, preferred_element_type=F32)
        cos_real, cos_imag = both[:STEP_ROWS, :PORTS], both[:STEP_ROWS, PORTS:]
        sin_real, sin_imag = both[STEP_ROWS:, :PORTS], both[STEP_ROWS:, PORTS:]
        plus.append((cos_real + sin_imag, cos_imag - sin_real))
        minus.append((cos_real - sin_imag, cos_imag + sin_real))
    phases = phases_ref[block].T
    quarter = HALF_PHIS // 2
    for theta in range(STEP_THETAS):
        low = theta * HALF_PHIS
        high = low + HALF_PHIS

        def along_y(face, part):
            return (plus[face][part][low:high], minus[face][part][low:high])

        def along_x(face, part):
            first, second = plus[face][part][low:high], minus[face][part][low:high]
            return (
                jnp.concatenate([first[quarter:], second[:quarter]], axis=0),
                jnp.concatenate([second[quarter:], first[:quarter]], axis=0),
            )

        kinds = (along_y, along_y, along_x, along_x)
        terms = [[kind(face, part) for part in (0, 1)] for face, kind in enumerate(kinds)]
        for half in range(2):
            start = theta * PHIS + half * HALF_PHIS
            cols = phases[start : start + HALF_PHIS]
            shared = [terms[0][part][half] + terms[2][part][half] for part in (0, 1)]
            real, imag = 0.0, 0.0
            for column, (re, im) in (
                (0, shared),
                (2, (terms[1][0][half], terms[1][1][half])),
                (4, (terms[3][0][half], terms[3][1][half])),
            ):
                cos, sin = cols[:, column : column + 1], cols[:, column + 1 : column + 2]
                real = real + cos * re + sin * im
                imag = imag + cos * im - sin * re
            rows = pl.ds(pl.multiple_of(step * STEP_DIRS + start, HALF_PHIS), HALF_PHIS)
            out_ref[rows, :PORTS] = real.astype(BF16)
            out_ref[rows, PORTS:] = imag.astype(BF16)


def call(kernel, name, inputs, outputs, scratch, in_space, out_space, flops, moved):
    return pl.pallas_call(
        kernel,
        out_shape=outputs,
        in_specs=[pl.BlockSpec(memory_space=in_space.get(i, VMEM)) for i in range(len(inputs))],
        out_specs=[pl.BlockSpec(memory_space=out_space.get(i, VMEM)) for i in range(len(outputs))],
        scratch_shapes=scratch,
        compiler_params=pltpu.CompilerParams(vmem_limit_bytes=VMEM_LIMIT),
        cost_estimate=pl.CostEstimate(flops=flops, bytes_accessed=moved, transcendentals=0),
        name=name,
    )(*inputs)


def shape(dims, dtype):
    return jax.ShapeDtypeStruct(dims, dtype)


def pairings(count):
    near = [(i, i ^ 1) for i in range(count)]
    far = [(i, (i + 1) % count if i % 2 else (i - 1) % count) for i in range(count)]
    return far, near


def exchange(axis, pair):
    permutations = pairings(lax.axis_size(axis))
    return [lax.ppermute(value, axis, permutation) for value, permutation in zip(pair, permutations)]


def phase_kernel(place_ref, cosines_ref, out_ref):
    factor = 1.0 / math.sqrt(ORDER * lax.axis_size("gx") * lax.axis_size("gy"))
    dir_x, dir_y = cosines_ref[:, 0], cosines_ref[:, 1]
    place_x, place_y = place_ref[0].astype(F32), place_ref[1].astype(F32)
    for index, (extra_x, extra_y) in enumerate(((0.0, 0.0), (SPACING, 0.0), (0.0, SPACING))):
        turns = ((place_x + extra_x) * dir_x + (place_y + extra_y) * dir_y) / WAVE
        angle = (turns - jnp.round(turns)) * (2.0 * math.pi)
        out_ref[:, 2 * index] = jnp.cos(angle) * factor
        out_ref[:, 2 * index + 1] = jnp.sin(angle) * factor
    for index in (6, 7):
        out_ref[:, index] = jnp.zeros((2 * STEPS, STEP_DIRS), F32)


def local(operator, incident, feed, port_element, positions):
    count_x, count_y = lax.axis_size("gx"), lax.axis_size("gy")
    half_flops = 2 * ORDER * ORDER * WIDE
    field_flops = 2 * ANGLES // 2 * FACE * WIDE * 4
    face_pair = [shape((FACE, WIDE), BF16)] * 2
    base_pair = shape((2, FACE, WIDE), F32)
    wide_bf16 = shape((ORDER, WIDE), BF16)
    oper, rhs, base_first, *sends = call(
        base_first_kernel,
        "base_first",
        [
            pltpu.with_memory_space_constraint(value, HBM)
            for value in (operator[0, 0], incident[0, 0], feed[0, 0], port_element.reshape(1, PORTS))
        ],
        [shape((4, 2, FACE, ORDER), BF16), wide_bf16, base_pair] + face_pair,
        [
            VMEM((2, ORDER, PORTS), BF16),
            VMEM((2, ORDER), BF16),
            VMEM((1, PORTS), jnp.int32),
            pltpu.SemaphoreType.DMA((4,)),
            pltpu.SemaphoreType.DMA((3,)),
        ],
        {0: HBM, 1: HBM, 2: HBM, 3: HBM},
        {},
        half_flops,
        10_000_000,
    )
    received = exchange("gy", sends)
    base_second, *sends = call(
        base_second_kernel, "base_second", (oper, rhs), [base_pair] + face_pair, [], {}, {}, half_flops, 5_000_000
    )
    received += exchange("gx", sends)
    for _ in range(ITERS - 1):
        *sends, trace = call(
            step_first_kernel,
            "step_first",
            (oper, base_first, *received),
            face_pair + [wide_bf16],
            [],
            {},
            {},
            half_flops,
            5_000_000,
        )
        received = exchange("gy", sends)
        sends = call(
            step_second_kernel,
            "step_second",
            (oper, base_second, trace),
            face_pair,
            [],
            {},
            {},
            half_flops,
            5_000_000,
        )
        received += exchange("gx", sends)
    (phases,) = call(
        phase_kernel,
        "phases",
        (positions.reshape(2), jnp.asarray(direction_cosines())),
        [shape((2 * STEPS, 8, STEP_DIRS), F32)],
        [],
        {0: pltpu.SMEM},
        {},
        1_000_000,
        100_000,
    )
    tables = jnp.asarray(face_tables())
    half_field = shape((ANGLES // 2, WIDE), BF16)
    currents, vec, theirs = call(
        last_kernel,
        "last",
        (oper, base_first, base_second, *received, tables, phases),
        [shape((2, ORDER, PORTS), BF16), wide_bf16, half_field],
        [VMEM((ORDER, WIDE), BF16), VMEM((2, ORDER, PORTS), BF16), pltpu.SemaphoreType.DMA],
        {},
        {0: HBM},
        2 * half_flops + field_flops,
        2_000_000,
    )
    theirs = lax.ppermute(theirs, "gx", [(i, i ^ 1) for i in range(count_x)])
    (mine,) = call(
        own_field_kernel, "own_field", (tables, phases, vec), [half_field], [], {}, {}, field_flops, 1_000_000
    )
    pair = (mine.astype(F32) + theirs.astype(F32)).astype(BF16)
    runs = 2
    length = count_y // runs
    across = [
        [i * count_y + run * length + at for i in range(parity, count_x, 2) for run in range(runs)]
        for parity in (0, 1)
        for at in range(length)
    ]
    along = [[run * length + at for at in range(length)] for run in range(runs)]
    members = len(across[0])
    pieces = lax.all_to_all(pair, ("gx", "gy"), 0, 0, tiled=True, axis_index_groups=across)
    column = jnp.sum(pieces.reshape(members, -1, WIDE).astype(F32), axis=0).astype(BF16)
    pieces = lax.all_to_all(column, "gy", 0, 0, tiled=True, axis_index_groups=along)
    pieces = pieces.reshape(length, -1, WIDE).astype(F32)
    fields = jnp.stack([jnp.sum(pieces[..., :PORTS], axis=0), jnp.sum(pieces[..., PORTS:], axis=0)], axis=1)
    return (currents[None, None], fields)


def solution(mesh):
    return jax.shard_map(
        local,
        mesh=mesh,
        in_specs=(
            P("gx", "gy", None, None, None),
            P("gx", "gy", None, None, None),
            P("gx", "gy", None, None),
            P(),
            P("gx", "gy", None),
        ),
        out_specs=(P("gx", "gy", None, None, None), P(("gx", "gy"), None, None)),
        check_vma=False,
    )
```

```python
import functools
import math

import jax
import jax.numpy as jnp
import ml_dtypes
import numpy as np
from jax import lax
from jax.experimental import pallas as pl
from jax.experimental.pallas import tpu as pltpu
from jax.sharding import PartitionSpec as P

THETAS = 32
PHIS = 64
ITERS = 3
SPACING = 8
WAVE = 2
FACE = 384
PORTS = 128
ORDER = 4 * FACE
WIDE = 2 * PORTS
ANGLES = THETAS * PHIS
HALF_PHIS = PHIS // 2
STEP_THETAS = 4
STEPS = THETAS // 2 // STEP_THETAS
STEP_ROWS = STEP_THETAS * HALF_PHIS
STEP_DIRS = STEP_THETAS * PHIS


VMEM = pltpu.VMEM
HBM = pltpu.HBM
VMEM_LIMIT = 16 << 20
UNROLL = 4
F32 = jnp.float32
BF16 = jnp.bfloat16


def theta_order():
    owner = np.arange(THETAS) // 2
    return [np.nonzero(owner % 2 == parity)[0] for parity in (0, 1)]


def face_tables():
    along = (np.arange(FACE) + 0.5) * (SPACING / FACE)
    sin_theta = np.sin((np.arange(THETAS) + 0.5) * (math.pi / (2.0 * THETAS)))
    sin_phi = np.sin(np.arange(HALF_PHIS) * (2.0 * math.pi / PHIS))
    angle = (2.0 * math.pi / WAVE) * (sin_theta[:, None] * sin_phi[None, :])[:, :, None] * along
    blocks = []
    for order in theta_order():
        for step in range(STEPS):
            part = angle[order[step * STEP_THETAS : (step + 1) * STEP_THETAS]]
            part = part.reshape(STEP_ROWS, FACE)
            blocks.append(np.concatenate([np.cos(part), np.sin(part)], axis=0))
    return np.stack(blocks).astype(ml_dtypes.bfloat16)


def direction_cosines():
    order = np.concatenate(theta_order())
    theta = (order + 0.5) * (math.pi / (2.0 * THETAS))
    azimuth = np.arange(PHIS) * (2.0 * math.pi / PHIS)
    dir_x = np.sin(theta)[:, None] * np.cos(azimuth)[None, :]
    dir_y = np.sin(theta)[:, None] * np.sin(azimuth)[None, :]
    whole = np.stack([dir_x.reshape(2 * STEPS, STEP_DIRS), dir_y.reshape(2 * STEPS, STEP_DIRS)], axis=1)
    return whole.astype(np.float32)


def swapped(vec):
    return jnp.concatenate([-vec[:, PORTS:], vec[:, :PORTS]], axis=1)


def faces_in_order():
    odd_x = lax.rem(lax.axis_index("gx"), 2)
    odd_y = lax.rem(lax.axis_index("gy"), 2)
    return (2 + odd_y, 3 - odd_y, odd_x, 1 - odd_x)


def face_rows(face):
    return pl.ds(pl.multiple_of(face * FACE, FACE), FACE)


def slot_product(oper_ref, slot, cols, vec, vec_swapped):
    return jnp.dot(oper_ref[slot, 0, :, cols], vec, preferred_element_type=F32) + jnp.dot(
        oper_ref[slot, 1, :, cols], vec_swapped, preferred_element_type=F32
    )


ALL_COLS = slice(0, ORDER)
NEAR_COLS = slice(0, 2 * FACE)
FAR_COLS = slice(2 * FACE, ORDER)


def base_first_kernel(oper_hbm, incident_hbm, feed_hbm, ports_hbm, oper_ref, rhs_ref, base_ref, *rest):
    outs, (incident, feed, ports, natural_ref, sems, small_sems) = rest[:2], rest[2:]
    faces = faces_in_order()
    columns = columns_in_order(faces)
    small = [
        pltpu.make_async_copy(source, target, small_sems.at[index])
        for index, (source, target) in enumerate(((incident_hbm, incident), (feed_hbm, feed), (ports_hbm, ports)))
    ]
    large = [operator_copies(oper_hbm, oper_ref, slot, face, columns, sems) for slot, face in enumerate(faces)]
    for copy in small + large[0] + large[1]:
        copy.start()
    for copy in small:
        copy.wait()
    myself = lax.axis_index("gx") * lax.axis_size("gy") + lax.axis_index("gy")
    selected = (ports[...] == myself).astype(F32).astype(BF16)
    blank = jnp.zeros_like(selected)
    select = jnp.concatenate(
        [jnp.concatenate([selected, blank], axis=1), jnp.concatenate([blank, selected], axis=1)], axis=0
    )
    fed = lax.dot_general(feed[...], select, (((0,), (0,)), ((), ())), preferred_element_type=F32)
    both = jnp.concatenate([incident[0], incident[1]], axis=1)
    natural_ref[...] = (both.astype(F32) + fed).astype(BF16)
    for index, face in enumerate(columns):
        rhs_ref[pl.ds(index * FACE, FACE), :] = natural_ref[face_rows(face), :]
    rhs = rhs_ref[...]
    rhs_swapped = swapped(rhs)
    for slot in range(2):
        for copy in large[slot]:
            copy.wait()
        for copy in large[slot + 2]:
            copy.start()
        base_slot(oper_ref, rhs, rhs_swapped, slot, base_ref, outs)
    for copy in large[2] + large[3]:
        copy.wait()


def columns_in_order(faces):
    return (faces[1], faces[3], faces[0], faces[2])


def column_of(slot):
    return (2, 0, 3, 1)[slot]


def operator_copies(oper_hbm, oper_ref, slot, face, columns, sems):
    return [
        pltpu.make_async_copy(
            oper_hbm.at[:, face_rows(face), face_rows(column)],
            oper_ref.at[slot, :, :, pl.ds(index * FACE, FACE)],
            sems.at[slot, index],
        )
        for index, column in enumerate(columns)
    ]


def base_slot(oper_ref, rhs, rhs_swapped, slot, base_ref, outs):
    start = column_of(slot) * FACE
    own = rhs[start : start + FACE].astype(F32)
    base = 0.5 * own + slot_product(oper_ref, slot, ALL_COLS, rhs, rhs_swapped)
    at = slot % len(outs)
    base_ref[at] = base
    outs[at][...] = (2.0 * base).astype(BF16)


def base_second_kernel(slot, oper_ref, rhs_ref, base_ref, out_ref):
    rhs = rhs_ref[...]
    base_slot(oper_ref, rhs, swapped(rhs), slot, base_ref, (out_ref,))


def joined(first_ref, second_ref):
    trace = jnp.concatenate([first_ref[...], second_ref[...]], axis=0)
    return trace, swapped(trace)


def near_kernel(oper_ref, base_first_ref, base_second_ref, base_third_ref, near_y_ref, near_x_ref, *outs):
    trace, trace_swapped = joined(near_y_ref, near_x_ref)
    for slot in range(4):
        base = (base_first_ref, base_first_ref, base_second_ref, base_third_ref)[slot][slot % 2 if slot < 2 else 0]
        outs[slot // 2][slot % 2] = base + slot_product(oper_ref, slot, NEAR_COLS, trace, trace_swapped)


def step_slots(oper_ref, part_ref, trace, trace_swapped, first, outs):
    for index in range(2):
        coupled = slot_product(oper_ref, first + index, FAR_COLS, trace, trace_swapped)
        outs[index][...] = (2.0 * (part_ref[index] + coupled)).astype(BF16)


def step_first_kernel(oper_ref, part_ref, far_y_ref, far_x_ref, first_ref, second_ref, trace_ref):
    trace, trace_swapped = joined(far_y_ref, far_x_ref)
    trace_ref[...] = trace
    step_slots(oper_ref, part_ref, trace, trace_swapped, 0, (first_ref, second_ref))


def step_second_kernel(slot, oper_ref, part_ref, trace_ref, out_ref):
    trace = trace_ref[...]
    coupled = slot_product(oper_ref, slot, FAR_COLS, trace, swapped(trace))
    out_ref[...] = (2.0 * (part_ref[slot - 2] + coupled)).astype(BF16)


def last_kernel(oper_ref, part_first_ref, part_second_ref, *rest):
    traces, tables_ref, phases_ref = rest[:4], rest[4], rest[5]
    currents_hbm, vec_ref, out_ref, split_ref, sem = rest[6:]
    trace, trace_swapped = joined(traces[0], traces[2])
    for slot, face in enumerate(faces_in_order()):
        rows = face_rows(face)
        part = (part_first_ref if slot < 2 else part_second_ref)[slot % 2]
        coupled = slot_product(oper_ref, slot, FAR_COLS, trace, trace_swapped)
        currents = (part + 0.5 * traces[slot][...].astype(F32) + coupled).astype(BF16)
        vec_ref[rows, :] = currents
        split_ref[0, rows, :] = currents[:, :PORTS]
        split_ref[1, rows, :] = currents[:, PORTS:]
    copy = pltpu.make_async_copy(split_ref, currents_hbm, sem)
    copy.start()
    field_steps(1 - lax.rem(lax.axis_index("gx"), 2), tables_ref, phases_ref, vec_ref, out_ref)
    copy.wait()


def own_field_kernel(tables_ref, phases_ref, vec_ref, out_ref):
    field_steps(lax.rem(lax.axis_index("gx"), 2), tables_ref, phases_ref, vec_ref, out_ref)


def field_steps(parity, tables_ref, phases_ref, vec_ref, out_ref):
    def body(step, carry):
        field_step(parity * STEPS + step, step, tables_ref, phases_ref, vec_ref, out_ref)
        return carry

    lax.fori_loop(0, STEPS, body, 0, unroll=UNROLL)


def field_step(block, step, tables_ref, phases_ref, vec_ref, out_ref):
    table = tables_ref[block]
    plus, minus = [], []
    for face in range(4):
        vec = vec_ref[pl.ds(face * FACE, FACE), :]
        both = jnp.dot(table, vec, preferred_element_type=F32)
        cos_real, cos_imag = both[:STEP_ROWS, :PORTS], both[:STEP_ROWS, PORTS:]
        sin_real, sin_imag = both[STEP_ROWS:, :PORTS], both[STEP_ROWS:, PORTS:]
        plus.append((cos_real + sin_imag, cos_imag - sin_real))
        minus.append((cos_real - sin_imag, cos_imag + sin_real))
    phases = phases_ref[block].T
    quarter = HALF_PHIS // 2
    for theta in range(STEP_THETAS):
        low = theta * HALF_PHIS
        high = low + HALF_PHIS

        def along_y(face, part):
            return (plus[face][part][low:high], minus[face][part][low:high])

        def along_x(face, part):
            first, second = plus[face][part][low:high], minus[face][part][low:high]
            return (
                jnp.concatenate([first[quarter:], second[:quarter]], axis=0),
                jnp.concatenate([second[quarter:], first[:quarter]], axis=0),
            )

        kinds = (along_y, along_y, along_x, along_x)
        terms = [[kind(face, part) for part in (0, 1)] for face, kind in enumerate(kinds)]
        for half in range(2):
            start = theta * PHIS + half * HALF_PHIS
            cols = phases[start : start + HALF_PHIS]
            shared = [terms[0][part][half] + terms[2][part][half] for part in (0, 1)]
            real, imag = 0.0, 0.0
            for column, (re, im) in (
                (0, shared),
                (2, (terms[1][0][half], terms[1][1][half])),
                (4, (terms[3][0][half], terms[3][1][half])),
            ):
                cos, sin = cols[:, column : column + 1], cols[:, column + 1 : column + 2]
                real = real + cos * re + sin * im
                imag = imag + cos * im - sin * re
            rows = pl.ds(pl.multiple_of(step * STEP_DIRS + start, HALF_PHIS), HALF_PHIS)
            out_ref[rows, :PORTS] = real.astype(BF16)
            out_ref[rows, PORTS:] = imag.astype(BF16)


def call(kernel, inputs, outputs, scratch, in_space, out_space, flops, moved):
    return pl.pallas_call(
        kernel,
        out_shape=outputs,
        in_specs=[pl.BlockSpec(memory_space=in_space.get(i, VMEM)) for i in range(len(inputs))],
        out_specs=[pl.BlockSpec(memory_space=out_space.get(i, VMEM)) for i in range(len(outputs))],
        scratch_shapes=scratch,
        compiler_params=pltpu.CompilerParams(vmem_limit_bytes=VMEM_LIMIT),
        cost_estimate=pl.CostEstimate(flops=flops, bytes_accessed=moved, transcendentals=0),
    )(*inputs)


def shape(dims, dtype):
    return jax.ShapeDtypeStruct(dims, dtype)


def pairings(count):
    near = [(i, i ^ 1) for i in range(count)]
    far = [(i, (i + 1) % count if i % 2 else (i - 1) % count) for i in range(count)]
    return far, near


def send(kind, axis, value):
    permutation = pairings(lax.axis_size(axis))[kind]
    return lax.ppermute(value, axis, permutation)


def exchange(first_sends, second_call):
    received = [send(kind, "gy", value) for kind, value in enumerate(first_sends)]
    rest = []
    for kind in range(2):
        value, *more = second_call(2 + kind)
        rest += more
        received.append(send(kind, "gx", value))
    return received, rest


def phase_kernel(place_ref, cosines_ref, out_ref):
    factor = 1.0 / math.sqrt(ORDER * lax.axis_size("gx") * lax.axis_size("gy"))
    dir_x, dir_y = cosines_ref[:, 0], cosines_ref[:, 1]
    place_x, place_y = place_ref[0].astype(F32), place_ref[1].astype(F32)
    for index, (extra_x, extra_y) in enumerate(((0.0, 0.0), (SPACING, 0.0), (0.0, SPACING))):
        turns = ((place_x + extra_x) * dir_x + (place_y + extra_y) * dir_y) / WAVE
        angle = (turns - jnp.round(turns)) * (2.0 * math.pi)
        out_ref[:, 2 * index] = jnp.cos(angle) * factor
        out_ref[:, 2 * index + 1] = jnp.sin(angle) * factor
    for index in (6, 7):
        out_ref[:, index] = jnp.zeros((2 * STEPS, STEP_DIRS), F32)


def local(operator, incident, feed, port_element, positions):
    count_x, count_y = lax.axis_size("gx"), lax.axis_size("gy")
    half_flops = 2 * ORDER * ORDER * WIDE
    field_flops = 2 * ANGLES // 2 * FACE * WIDE * 4
    face_pair = [shape((FACE, WIDE), BF16)] * 2
    base_pair = shape((2, FACE, WIDE), F32)
    wide_bf16 = shape((ORDER, WIDE), BF16)
    oper, rhs, base_first, *sends = call(
        base_first_kernel,
        [
            pltpu.with_memory_space_constraint(value, HBM)
            for value in (operator[0, 0], incident[0, 0], feed[0, 0], port_element.reshape(1, PORTS))
        ],
        [shape((4, 2, FACE, ORDER), BF16), wide_bf16, base_pair] + face_pair,
        [
            VMEM((2, ORDER, PORTS), BF16),
            VMEM((2, ORDER), BF16),
            VMEM((1, PORTS), jnp.int32),
            VMEM((ORDER, WIDE), BF16),
            pltpu.SemaphoreType.DMA((4, 4)),
            pltpu.SemaphoreType.DMA((3,)),
        ],
        {0: HBM, 1: HBM, 2: HBM, 3: HBM},
        {},
        half_flops,
        10_000_000,
    )

    def second_base(slot):
        base, out = call(
            functools.partial(base_second_kernel, slot),
            (oper, rhs),
            [shape((1, FACE, WIDE), F32), face_pair[0]],
            [],
            {},
            {},
            half_flops // 2,
            2_500_000,
        )
        return out, base

    received, bases = exchange(sends, second_base)
    far_bf16 = shape((2 * FACE, WIDE), BF16)

    def near_part(received):
        return call(
            near_kernel,
            (oper, base_first, *bases, received[1], received[3]),
            [base_pair] * 2,
            [],
            {},
            {},
            half_flops,
            5_000_000,
        )

    for _ in range(1, ITERS):
        part_first, part_second = near_part(received)
        *sends, trace = call(
            step_first_kernel,
            (oper, part_first, received[0], received[2]),
            face_pair + [far_bf16],
            [],
            {},
            {},
            half_flops // 2,
            2_500_000,
        )
        received, _ = exchange(
            sends,
            lambda slot: call(
                functools.partial(step_second_kernel, slot),
                (oper, part_second, trace),
                face_pair[:1],
                [],
                {},
                {},
                half_flops // 4,
                1_250_000,
            ),
        )
    part_first, part_second = near_part(received)
    (phases,) = call(
        phase_kernel,
        (positions.reshape(2), jnp.asarray(direction_cosines())),
        [shape((2 * STEPS, 8, STEP_DIRS), F32)],
        [],
        {0: pltpu.SMEM},
        {},
        1_000_000,
        100_000,
    )
    tables = jnp.asarray(face_tables())
    half_field = shape((ANGLES // 2, WIDE), BF16)
    currents, vec, theirs = call(
        last_kernel,
        (oper, part_first, part_second, *received, tables, phases),
        [shape((2, ORDER, PORTS), BF16), wide_bf16, half_field],
        [VMEM((2, ORDER, PORTS), BF16), pltpu.SemaphoreType.DMA],
        {},
        {0: HBM},
        half_flops + field_flops,
        2_000_000,
    )
    theirs = lax.ppermute(theirs, "gx", [(i, i ^ 1) for i in range(count_x)])
    (mine,) = call(own_field_kernel, (tables, phases, vec), [half_field], [], {}, {}, field_flops, 1_000_000)
    pair = (mine.astype(F32) + theirs.astype(F32)).astype(BF16)
    runs = 2
    length = count_y // runs
    across = [
        [i * count_y + run * length + at for i in range(parity, count_x, 2) for run in range(runs)]
        for parity in (0, 1)
        for at in range(length)
    ]
    along = [[run * length + at for at in range(length)] for run in range(runs)]
    members = len(across[0])
    pieces = lax.all_to_all(pair, ("gx", "gy"), 0, 0, tiled=True, axis_index_groups=across)
    column = jnp.sum(pieces.reshape(members, -1, WIDE).astype(F32), axis=0).astype(BF16)
    pieces = lax.all_to_all(column, "gy", 0, 0, tiled=True, axis_index_groups=along)
    pieces = pieces.reshape(length, -1, WIDE).astype(F32)
    fields = jnp.stack([jnp.sum(pieces[..., :PORTS], axis=0), jnp.sum(pieces[..., PORTS:], axis=0)], axis=1)
    return (currents[None, None], fields)


def solution(mesh):
    return jax.shard_map(
        local,
        mesh=mesh,
        in_specs=(
            P("gx", "gy", None, None, None),
            P("gx", "gy", None, None, None),
            P("gx", "gy", None, None),
            P(),
            P("gx", "gy", None),
        ),
        out_specs=(P("gx", "gy", None, None, None), P(("gx", "gy"), None, None)),
        check_vma=False,
    )
```

```python
import functools
import math

import jax
import jax.numpy as jnp
import ml_dtypes
import numpy as np
from jax import lax
from jax.experimental import pallas as pl
from jax.experimental.pallas import tpu as pltpu
from jax.sharding import PartitionSpec as P

THETAS = 32
PHIS = 64
ITERS = 3
SPACING = 8
WAVE = 2
FACE = 384
PORTS = 128
ORDER = 4 * FACE
WIDE = 2 * PORTS
ANGLES = THETAS * PHIS
HALF_PHIS = PHIS // 2
STEP_THETAS = 4
STEPS = THETAS // 2 // STEP_THETAS
STEP_ROWS = STEP_THETAS * HALF_PHIS
STEP_DIRS = STEP_THETAS * PHIS


VMEM = pltpu.VMEM
HBM = pltpu.HBM
VMEM_LIMIT = 16 << 20
UNROLL = 4
F32 = jnp.float32
BF16 = jnp.bfloat16


def theta_order():
    owner = np.arange(THETAS) // 2
    return [np.nonzero(owner % 2 == parity)[0] for parity in (0, 1)]


def face_tables():
    along = (np.arange(FACE) + 0.5) * (SPACING / FACE)
    sin_theta = np.sin((np.arange(THETAS) + 0.5) * (math.pi / (2.0 * THETAS)))
    sin_phi = np.sin(np.arange(HALF_PHIS) * (2.0 * math.pi / PHIS))
    angle = (2.0 * math.pi / WAVE) * (sin_theta[:, None] * sin_phi[None, :])[:, :, None] * along
    blocks = []
    for order in theta_order():
        for step in range(STEPS):
            part = angle[order[step * STEP_THETAS : (step + 1) * STEP_THETAS]]
            part = part.reshape(STEP_ROWS, FACE)
            blocks.append(np.concatenate([np.cos(part), np.sin(part)], axis=0))
    return np.stack(blocks).astype(ml_dtypes.bfloat16)


def direction_cosines():
    order = np.concatenate(theta_order())
    theta = (order + 0.5) * (math.pi / (2.0 * THETAS))
    azimuth = np.arange(PHIS) * (2.0 * math.pi / PHIS)
    dir_x = np.sin(theta)[:, None] * np.cos(azimuth)[None, :]
    dir_y = np.sin(theta)[:, None] * np.sin(azimuth)[None, :]
    whole = np.stack([dir_x.reshape(2 * STEPS, STEP_DIRS), dir_y.reshape(2 * STEPS, STEP_DIRS)], axis=1)
    return whole.astype(np.float32)


def swapped(vec):
    return jnp.concatenate([-vec[:, PORTS:], vec[:, :PORTS]], axis=1)


def faces_in_order():
    odd_x = lax.rem(lax.axis_index("gx"), 2)
    odd_y = lax.rem(lax.axis_index("gy"), 2)
    return (2 + odd_y, 3 - odd_y, odd_x, 1 - odd_x)


def face_rows(face):
    return pl.ds(pl.multiple_of(face * FACE, FACE), FACE)


def slot_product(oper_ref, slot, cols, vec, vec_swapped):
    return jnp.dot(oper_ref[slot, 0, :, cols], vec, preferred_element_type=F32) + jnp.dot(
        oper_ref[slot, 1, :, cols], vec_swapped, preferred_element_type=F32
    )


ALL_COLS = slice(0, ORDER)
NEAR_COLS = slice(0, 2 * FACE)
FAR_COLS = slice(2 * FACE, ORDER)
FAR_Y_COLS = slice(2 * FACE, 3 * FACE)
FAR_X_COLS = slice(3 * FACE, ORDER)


def base_first_kernel(oper_hbm, incident_hbm, feed_hbm, ports_hbm, oper_ref, rhs_ref, base_ref, *rest):
    outs, (incident, feed, ports, natural_ref, sems, small_sems) = rest[:2], rest[2:]
    faces = faces_in_order()
    columns = columns_in_order(faces)
    small = [
        pltpu.make_async_copy(source, target, small_sems.at[index])
        for index, (source, target) in enumerate(((incident_hbm, incident), (feed_hbm, feed), (ports_hbm, ports)))
    ]
    large = [operator_copies(oper_hbm, oper_ref, slot, face, columns, sems) for slot, face in enumerate(faces)]
    for copy in small + large[0] + large[1]:
        copy.start()
    for copy in small:
        copy.wait()
    myself = lax.axis_index("gx") * lax.axis_size("gy") + lax.axis_index("gy")
    selected = (ports[...] == myself).astype(F32).astype(BF16)
    blank = jnp.zeros_like(selected)
    select = jnp.concatenate(
        [jnp.concatenate([selected, blank], axis=1), jnp.concatenate([blank, selected], axis=1)], axis=0
    )
    fed = lax.dot_general(feed[...], select, (((0,), (0,)), ((), ())), preferred_element_type=F32)
    both = jnp.concatenate([incident[0], incident[1]], axis=1)
    natural_ref[...] = (both.astype(F32) + fed).astype(BF16)
    for index, face in enumerate(columns):
        rhs_ref[pl.ds(index * FACE, FACE), :] = natural_ref[face_rows(face), :]
    rhs = rhs_ref[...]
    rhs_swapped = swapped(rhs)
    for slot in range(2):
        for copy in large[slot]:
            copy.wait()
        for copy in large[slot + 2]:
            copy.start()
        base_slot(oper_ref, rhs, rhs_swapped, slot, base_ref, outs)
    for copy in large[2] + large[3]:
        copy.wait()


def columns_in_order(faces):
    return (faces[1], faces[3], faces[0], faces[2])


def column_of(slot):
    return (2, 0, 3, 1)[slot]


def operator_copies(oper_hbm, oper_ref, slot, face, columns, sems):
    return [
        pltpu.make_async_copy(
            oper_hbm.at[:, face_rows(face), face_rows(column)],
            oper_ref.at[slot, :, :, pl.ds(index * FACE, FACE)],
            sems.at[slot, index],
        )
        for index, column in enumerate(columns)
    ]


def base_slot(oper_ref, rhs, rhs_swapped, slot, base_ref, outs):
    start = column_of(slot) * FACE
    own = rhs[start : start + FACE].astype(F32)
    base = 0.5 * own + slot_product(oper_ref, slot, ALL_COLS, rhs, rhs_swapped)
    at = slot % len(outs)
    base_ref[at] = base
    outs[at][...] = (2.0 * base).astype(BF16)


def base_second_kernel(slot, oper_ref, rhs_ref, base_ref, out_ref):
    rhs = rhs_ref[...]
    base_slot(oper_ref, rhs, swapped(rhs), slot, base_ref, (out_ref,))


def joined(first_ref, second_ref):
    trace = jnp.concatenate([first_ref[...], second_ref[...]], axis=0)
    return trace, swapped(trace)


def near_kernel(oper_ref, base_first_ref, base_second_ref, base_third_ref, near_y_ref, near_x_ref, *outs):
    trace, trace_swapped = joined(near_y_ref, near_x_ref)
    for slot in range(4):
        base = (base_first_ref, base_first_ref, base_second_ref, base_third_ref)[slot][slot % 2 if slot < 2 else 0]
        outs[slot // 2][slot % 2] = base + slot_product(oper_ref, slot, NEAR_COLS, trace, trace_swapped)


def step_slots(oper_ref, part_ref, trace, trace_swapped, first, outs):
    for index in range(2):
        coupled = slot_product(oper_ref, first + index, FAR_COLS, trace, trace_swapped)
        outs[index][...] = (2.0 * (part_ref[index] + coupled)).astype(BF16)


def step_first_kernel(oper_ref, part_ref, far_y_ref, far_x_ref, first_ref, second_ref, trace_ref):
    trace, trace_swapped = joined(far_y_ref, far_x_ref)
    trace_ref[...] = trace
    step_slots(oper_ref, part_ref, trace, trace_swapped, 0, (first_ref, second_ref))


def step_second_kernel(slot, oper_ref, part_ref, trace_ref, out_ref):
    trace = trace_ref[...]
    coupled = slot_product(oper_ref, slot, FAR_COLS, trace, swapped(trace))
    out_ref[...] = (2.0 * (part_ref[slot - 2] + coupled)).astype(BF16)


def far_y_kernel(oper_ref, part_first_ref, part_second_ref, far_y_ref, *outs):
    trace = far_y_ref[...]
    trace_swapped = swapped(trace)
    for slot in range(4):
        part = (part_first_ref if slot < 2 else part_second_ref)[slot % 2]
        outs[slot // 2][slot % 2] = part + slot_product(oper_ref, slot, FAR_Y_COLS, trace, trace_swapped)


def last_kernel(oper_ref, part_first_ref, part_second_ref, *rest):
    traces, tables_ref, phases_ref = rest[:4], rest[4], rest[5]
    currents_hbm, vec_ref, out_ref, split_ref, sem = rest[6:]
    trace = traces[2][...]
    trace_swapped = swapped(trace)
    for slot, face in enumerate(faces_in_order()):
        rows = face_rows(face)
        part = (part_first_ref if slot < 2 else part_second_ref)[slot % 2]
        coupled = slot_product(oper_ref, slot, FAR_X_COLS, trace, trace_swapped)
        currents = (part + 0.5 * traces[slot][...].astype(F32) + coupled).astype(BF16)
        vec_ref[rows, :] = currents
        split_ref[0, rows, :] = currents[:, :PORTS]
        split_ref[1, rows, :] = currents[:, PORTS:]
    copy = pltpu.make_async_copy(split_ref, currents_hbm, sem)
    copy.start()
    field_steps(1 - lax.rem(lax.axis_index("gx"), 2), tables_ref, phases_ref, vec_ref, out_ref)
    copy.wait()


def own_field_kernel(tables_ref, phases_ref, vec_ref, out_ref):
    field_steps(lax.rem(lax.axis_index("gx"), 2), tables_ref, phases_ref, vec_ref, out_ref)


def field_steps(parity, tables_ref, phases_ref, vec_ref, out_ref):
    def body(step, carry):
        field_step(parity * STEPS + step, step, tables_ref, phases_ref, vec_ref, out_ref)
        return carry

    lax.fori_loop(0, STEPS, body, 0, unroll=UNROLL)


def field_step(block, step, tables_ref, phases_ref, vec_ref, out_ref):
    table = tables_ref[block]
    plus, minus = [], []
    for face in range(4):
        vec = vec_ref[pl.ds(face * FACE, FACE), :]
        both = jnp.dot(table, vec, preferred_element_type=F32)
        cos_real, cos_imag = both[:STEP_ROWS, :PORTS], both[:STEP_ROWS, PORTS:]
        sin_real, sin_imag = both[STEP_ROWS:, :PORTS], both[STEP_ROWS:, PORTS:]
        plus.append((cos_real + sin_imag, cos_imag - sin_real))
        minus.append((cos_real - sin_imag, cos_imag + sin_real))
    phases = phases_ref[block].T
    quarter = HALF_PHIS // 2
    for theta in range(STEP_THETAS):
        low = theta * HALF_PHIS
        high = low + HALF_PHIS

        def along_y(face, part):
            return (plus[face][part][low:high], minus[face][part][low:high])

        def along_x(face, part):
            first, second = plus[face][part][low:high], minus[face][part][low:high]
            return (
                jnp.concatenate([first[quarter:], second[:quarter]], axis=0),
                jnp.concatenate([second[quarter:], first[:quarter]], axis=0),
            )

        kinds = (along_y, along_y, along_x, along_x)
        terms = [[kind(face, part) for part in (0, 1)] for face, kind in enumerate(kinds)]
        for half in range(2):
            start = theta * PHIS + half * HALF_PHIS
            cols = phases[start : start + HALF_PHIS]
            shared = [terms[0][part][half] + terms[2][part][half] for part in (0, 1)]
            real, imag = 0.0, 0.0
            for column, (re, im) in (
                (0, shared),
                (2, (terms[1][0][half], terms[1][1][half])),
                (4, (terms[3][0][half], terms[3][1][half])),
            ):
                cos, sin = cols[:, column : column + 1], cols[:, column + 1 : column + 2]
                real = real + cos * re + sin * im
                imag = imag + cos * im - sin * re
            rows = pl.ds(pl.multiple_of(step * STEP_DIRS + start, HALF_PHIS), HALF_PHIS)
            out_ref[rows, :PORTS] = real.astype(BF16)
            out_ref[rows, PORTS:] = imag.astype(BF16)


def call(kernel, inputs, outputs, scratch, in_space, out_space, flops, moved):
    return pl.pallas_call(
        kernel,
        out_shape=outputs,
        in_specs=[pl.BlockSpec(memory_space=in_space.get(i, VMEM)) for i in range(len(inputs))],
        out_specs=[pl.BlockSpec(memory_space=out_space.get(i, VMEM)) for i in range(len(outputs))],
        scratch_shapes=scratch,
        compiler_params=pltpu.CompilerParams(vmem_limit_bytes=VMEM_LIMIT),
        cost_estimate=pl.CostEstimate(flops=flops, bytes_accessed=moved, transcendentals=0),
    )(*inputs)


def shape(dims, dtype):
    return jax.ShapeDtypeStruct(dims, dtype)


def pairings(count):
    near = [(i, i ^ 1) for i in range(count)]
    far = [(i, (i + 1) % count if i % 2 else (i - 1) % count) for i in range(count)]
    return far, near


def send(kind, axis, value):
    permutation = pairings(lax.axis_size(axis))[kind]
    return lax.ppermute(value, axis, permutation)


def exchange(first_sends, second_call):
    received = [send(kind, "gy", value) for kind, value in enumerate(first_sends)]
    rest = []
    for kind in range(2):
        value, *more = second_call(2 + kind)
        rest += more
        received.append(send(kind, "gx", value))
    return received, rest


def phase_kernel(place_ref, cosines_ref, out_ref):
    factor = 1.0 / math.sqrt(ORDER * lax.axis_size("gx") * lax.axis_size("gy"))
    dir_x, dir_y = cosines_ref[:, 0], cosines_ref[:, 1]
    place_x, place_y = place_ref[0].astype(F32), place_ref[1].astype(F32)
    for index, (extra_x, extra_y) in enumerate(((0.0, 0.0), (SPACING, 0.0), (0.0, SPACING))):
        turns = ((place_x + extra_x) * dir_x + (place_y + extra_y) * dir_y) / WAVE
        angle = (turns - jnp.round(turns)) * (2.0 * math.pi)
        out_ref[:, 2 * index] = jnp.cos(angle) * factor
        out_ref[:, 2 * index + 1] = jnp.sin(angle) * factor
    for index in (6, 7):
        out_ref[:, index] = jnp.zeros((2 * STEPS, STEP_DIRS), F32)


def local(operator, incident, feed, port_element, positions):
    count_x, count_y = lax.axis_size("gx"), lax.axis_size("gy")
    half_flops = 2 * ORDER * ORDER * WIDE
    field_flops = 2 * ANGLES // 2 * FACE * WIDE * 4
    face_pair = [shape((FACE, WIDE), BF16)] * 2
    base_pair = shape((2, FACE, WIDE), F32)
    wide_bf16 = shape((ORDER, WIDE), BF16)
    oper, rhs, base_first, *sends = call(
        base_first_kernel,
        [
            pltpu.with_memory_space_constraint(value, HBM)
            for value in (operator[0, 0], incident[0, 0], feed[0, 0], port_element.reshape(1, PORTS))
        ],
        [shape((4, 2, FACE, ORDER), BF16), wide_bf16, base_pair] + face_pair,
        [
            VMEM((2, ORDER, PORTS), BF16),
            VMEM((2, ORDER), BF16),
            VMEM((1, PORTS), jnp.int32),
            VMEM((ORDER, WIDE), BF16),
            pltpu.SemaphoreType.DMA((4, 4)),
            pltpu.SemaphoreType.DMA((3,)),
        ],
        {0: HBM, 1: HBM, 2: HBM, 3: HBM},
        {},
        half_flops,
        10_000_000,
    )

    def second_base(slot):
        base, out = call(
            functools.partial(base_second_kernel, slot),
            (oper, rhs),
            [shape((1, FACE, WIDE), F32), face_pair[0]],
            [],
            {},
            {},
            half_flops // 2,
            2_500_000,
        )
        return out, base

    received, bases = exchange(sends, second_base)
    far_bf16 = shape((2 * FACE, WIDE), BF16)

    def near_part(received):
        return call(
            near_kernel,
            (oper, base_first, *bases, received[1], received[3]),
            [base_pair] * 2,
            [],
            {},
            {},
            half_flops,
            5_000_000,
        )

    for _ in range(1, ITERS):
        part_first, part_second = near_part(received)
        *sends, trace = call(
            step_first_kernel,
            (oper, part_first, received[0], received[2]),
            face_pair + [far_bf16],
            [],
            {},
            {},
            half_flops // 2,
            2_500_000,
        )
        received, _ = exchange(
            sends,
            lambda slot: call(
                functools.partial(step_second_kernel, slot),
                (oper, part_second, trace),
                face_pair[:1],
                [],
                {},
                {},
                half_flops // 4,
                1_250_000,
            ),
        )
    part_first, part_second = near_part(received)
    part_first, part_second = call(
        far_y_kernel,
        (oper, part_first, part_second, received[0]),
        [base_pair] * 2,
        [],
        {},
        {},
        half_flops // 2,
        2_500_000,
    )
    (phases,) = call(
        phase_kernel,
        (positions.reshape(2), jnp.asarray(direction_cosines())),
        [shape((2 * STEPS, 8, STEP_DIRS), F32)],
        [],
        {0: pltpu.SMEM},
        {},
        1_000_000,
        100_000,
    )
    tables = jnp.asarray(face_tables())
    half_field = shape((ANGLES // 2, WIDE), BF16)
    currents, vec, theirs = call(
        last_kernel,
        (oper, part_first, part_second, *received, tables, phases),
        [shape((2, ORDER, PORTS), BF16), wide_bf16, half_field],
        [VMEM((2, ORDER, PORTS), BF16), pltpu.SemaphoreType.DMA],
        {},
        {0: HBM},
        half_flops + field_flops,
        2_000_000,
    )
    theirs = lax.ppermute(theirs, "gx", [(i, i ^ 1) for i in range(count_x)])
    (mine,) = call(own_field_kernel, (tables, phases, vec), [half_field], [], {}, {}, field_flops, 1_000_000)
    pair = (mine.astype(F32) + theirs.astype(F32)).astype(BF16)
    runs = 2
    length = count_y // runs
    across = [
        [i * count_y + run * length + at for i in range(parity, count_x, 2) for run in range(runs)]
        for parity in (0, 1)
        for at in range(length)
    ]
    along = [[run * length + at for at in range(length)] for run in range(runs)]
    members = len(across[0])
    pieces = lax.all_to_all(pair, ("gx", "gy"), 0, 0, tiled=True, axis_index_groups=across)
    column = jnp.sum(pieces.reshape(members, -1, WIDE).astype(F32), axis=0).astype(BF16)
    pieces = lax.all_to_all(column, "gy", 0, 0, tiled=True, axis_index_groups=along)
    pieces = pieces.reshape(length, -1, WIDE).astype(F32)
    fields = jnp.stack([jnp.sum(pieces[..., :PORTS], axis=0), jnp.sum(pieces[..., PORTS:], axis=0)], axis=1)
    return (currents[None, None], fields)


def solution(mesh):
    return jax.shard_map(
        local,
        mesh=mesh,
        in_specs=(
            P("gx", "gy", None, None, None),
            P("gx", "gy", None, None, None),
            P("gx", "gy", None, None),
            P(),
            P("gx", "gy", None),
        ),
        out_specs=(P("gx", "gy", None, None, None), P(("gx", "gy"), None, None)),
        check_vma=False,
    )
```
